32 devices in a mesh: dp: 8 (over z, y), mp: 4 (over x, core).
Axes of the slice: x: 2, y: 2, z: 4, core: 2. Of those that a mesh axis runs over, the one named last changes fastest.
Arguments:
- hidden_in: bfloat16 [16384, 2048], P('dp', 'mp'), may hold values from -18 to 18
- cotangent: bfloat16 [16384, 2048], P('dp', 'mp'), may hold values from -6 to 6
- segment_ids: int32 [16, 1024], P('dp'), may hold values from 0 to 15, never falling along the last dimension, each value on 1 to 512 neighbouring positions
- adapter_ids: int32 [16], P('dp'), may hold values from 0 to 7
- ln_gain: float32 [2048], replicated, may hold values from 0.5 to 1.5
- ln_bias: float32 [2048], replicated, may hold values from -4 to 4
- w_qkv: bfloat16 [2048, 3, 2048], P('dp', None, 'mp'), may hold values from -0.125 to 0.125
- b_qkv: bfloat16 [3, 2048], P(None, 'mp'), may hold values from -4 to 4
- w_out: bfloat16 [2048, 2048], P('mp', 'dp'), may hold values from -0.375 to 0.375
- b_out: bfloat16 [2048], P('mp'), may hold values from -4 to 4
- w_fc1: bfloat16 [2048, 8192], P('dp', 'mp'), may hold values from -0.125 to 0.125
- b_fc1: bfloat16 [8192], P('mp'), may hold values from -4 to 4
- w_fc2: bfloat16 [8192, 2048], P('mp', 'dp'), may hold values from -0.0625 to 0.0625
- b_fc2: bfloat16 [2048], P('mp'), may hold values from -4 to 4
- down_input_factors: bfloat16 [8, 4, 16, 2048], P(None, None, None, 'dp'), may hold values from -0.125 to 0.125
- up_qkv: bfloat16 [8, 16, 3, 2048], P(None, 'dp', None, 'mp'), may hold values from -1.5 to 1.5
- up_fc1: bfloat16 [8, 16, 8192], P(None, 'dp', 'mp'), may hold values from -1.5 to 1.5
- down_o: bfloat16 [8, 16, 2048], P(None, 'dp', 'mp'), may hold values from -0.375 to 0.375
- down_fc2: bfloat16 [8, 16, 8192], P(None, 'dp', 'mp'), may hold values from -0.0625 to 0.0625
- up_output_factors: bfloat16 [8, 2, 16, 2048], P(None, None, 'dp', 'mp'), may hold values from -3 to 3
Outputs:
- output: bfloat16 [16384, 2048], P('dp', 'mp')
- grad_in: bfloat16 [16384, 2048], P('dp', 'mp')
- grad_down_x: float32 [8, 4, 16, 2048], P(None, None, None, 'dp')
- grad_up_qkv: float32 [8, 16, 3, 2048], P(None, 'dp', None, 'mp')
- grad_up_fc1: float32 [8, 16, 8192], P(None, 'dp', 'mp')
- grad_down_o: float32 [8, 16, 2048], P(None, 'dp', 'mp')
- grad_down_fc2: float32 [8, 16, 8192], P(None, 'dp', 'mp')
- grad_up_out: float32 [8, 2, 16, 2048], P(None, None, 'dp', 'mp')
The draws below stay inside these ranges and needn't reach their ends.
Inputs may be any that keep to these rules, and one draw needn't show every extreme that they name: `segment_ids`: within a sequence the ids never fall; a document is a run of equal ids.
All inputs are finite; a program needn't handle non-finite values.
Results may differ from the reference program's by a relative error of at most 0.0094.
Values may be sent and summed in bfloat16 or wider, within the bound.
No kernel may reach another device: no remote copies, remote signals or barrier semaphores. Data moves between devices by JAX's collectives and lax.ppermute only.
A program may use at most 320 MiB of HBM per device.

```python
import math
import jax
import jax.numpy as jnp
import numpy as np
from jax import lax

MODEL_WIDTH = 2048
HEADS = 32
HEAD_DIM = 64
ROT = 32
FF = 8192
R = 16
NAD = 8
LEN = 1024
DOCS = 16
SEQ_DEV = 2
HD = 2048
SEQS = 16
TOKENS_PER_SHARD = 2048
TOKENS = 16384
N_DP = 8


def draw_hidden_in(key, part):
    row_key, entry_key = jax.random.split(key, 2)
    row_scale = jnp.exp(jax.random.uniform(row_key, (TOKENS, 1), jnp.float32, math.log(0.5), math.log(5.0)))
    entries = jnp.clip(jax.random.normal(entry_key, (TOKENS, MODEL_WIDTH), jnp.float32), -3.5, 3.5)
    return (row_scale * entries).astype(jnp.bfloat16)


def touch_ends(values, rng, least, top_value):
    longest = values.shape.index(max(values.shape))
    spots = []
    for shift in (0, 1):
        where = [jax.random.randint(jax.random.fold_in(rng, axis), (), 0, length) for axis, length in enumerate(values.shape)]
        where[longest] = (where[longest] + shift) % values.shape[longest]
        spots.append(tuple(where))
    return values.at[spots[0]].set(least).at[spots[1]].set(top_value)


def levels(key, dims, cuts, low, high):
    def one(axis_at, shards_of):
        heights = jax.random.uniform(jax.random.fold_in(jax.random.fold_in(key, 6), axis_at), (shards_of,), jnp.float32, low / len(cuts), high / len(cuts))
        return jnp.repeat(jnp.exp(heights), dims[axis_at] // shards_of).reshape((-1,) + (1,) * (len(dims) - axis_at - 1))

    factor_of = one(*cuts[0])
    for cut in cuts[1:]:
        factor_of = factor_of * one(*cut)
    return factor_of


def profile(number_of, total, most, skew):
    weights = [(1 << 20) // math.isqrt(rank ** skew) + 1 for rank in range(2, number_of + 1)]
    spare, given = total - most - (number_of - 1), [1] * (number_of - 1)
    while spare > 0:
        candidates = [i for i in range(number_of - 1) if given[i] < most]
        pool, left = sum([weights[i] for i in candidates]), spare
        for i in candidates:
            addition = min(most - given[i], max(1, left * weights[i] // pool), spare)
            given[i] = given[i] + addition
            spare = spare - addition
    return np.array([most] + given)


def uneven(rng, count, total, bound, skew):
    if count == 2:
        one = jax.random.randint(rng, (), max(1, total - bound), min(bound, total - 1) + 1)
        return jnp.stack([one, total - one])
    sizes = jnp.asarray(profile(count, total, bound, skew), jnp.int32)
    twos = (count - 1) // 2
    source_of, taker = sizes[1:1 + 2 * twos:2], sizes[2:2 + 2 * twos:2]
    margin = jnp.minimum(source_of - 1, bound - taker)
    passed = jax.random.randint(jax.random.fold_in(rng, 1), (twos,), 0, 1 << 20) % (margin + 1)
    sizes = sizes.at[1:1 + 2 * twos:2].set(source_of - passed).at[2:2 + 2 * twos:2].set(taker + passed)
    return sizes[jax.random.permutation(jax.random.fold_in(rng, 2), count)]


def bell_draw(stream_key, shape, spread, limit, shards=(), kind=jnp.bfloat16):
    values = spread * jax.random.normal(stream_key, shape, jnp.float32)
    if shards:
        values = values * levels(stream_key, shape, shards, -0.22, 0.18)
    return jnp.clip(values, -limit, limit).astype(kind)


def setup_inputs(seed: int = 0) -> dict:
    keys = jax.random.split(jax.random.key(seed), 21)
    return {
        "hidden_in": draw_hidden_in(jax.random.fold_in(keys[20], 71), 0),
        "cotangent": bell_draw(keys[1], (TOKENS, MODEL_WIDTH), 1.0, 6.0, ((0, 8), (1, 4))),
        "segment_ids": jax.vmap(lambda own: jnp.searchsorted(jnp.cumsum(uneven(own, DOCS, LEN, LEN // 2, 2)), jnp.arange(LEN), side="right"))(jax.random.split(keys[2], SEQS)).reshape((SEQS, LEN)).astype(jnp.int32),
        "adapter_ids": touch_ends(jax.random.randint(keys[3], (SEQS,), 0, NAD), jax.random.fold_in(keys[3], 1), 0, NAD - 1).astype(jnp.int32),
        "ln_gain": jnp.clip(1.0 + 0.1 * jax.random.normal(keys[4], (MODEL_WIDTH,), jnp.float32), 0.5, 1.5),
        "ln_bias": bell_draw(keys[5], (MODEL_WIDTH,), 0.3, 4.0, (), jnp.float32),
        "w_qkv": bell_draw(keys[6], (MODEL_WIDTH, 3, HD), MODEL_WIDTH ** -0.5, 0.125, ((0, 8), (2, 4))),
        "b_qkv": bell_draw(keys[7], (3, HD), 0.3, 4.0, ((1, 4),)),
        "w_out": bell_draw(keys[8], (HD, MODEL_WIDTH), (HD // 8) ** -0.5, 0.375, ((0, 4), (1, 8))),
        "b_out": bell_draw(keys[9], (MODEL_WIDTH,), 0.3, 4.0, ((0, 4),)),
        "w_fc1": bell_draw(keys[10], (MODEL_WIDTH, FF), MODEL_WIDTH ** -0.5, 0.125, ((0, 8), (1, 4))),
        "b_fc1": bell_draw(keys[11], (FF,), 0.3, 4.0, ((0, 4),)),
        "w_fc2": bell_draw(keys[12], (FF, MODEL_WIDTH), FF ** -0.5, 0.0625, ((0, 4), (1, 8))),
        "b_fc2": bell_draw(keys[13], (MODEL_WIDTH,), 0.3, 4.0, ((0, 4),)),
        "down_input_factors": bell_draw(keys[14], (NAD, 4, R, MODEL_WIDTH), MODEL_WIDTH ** -0.5, 0.125, ((3, 8),)),
        "up_qkv": bell_draw(keys[15], (NAD, R, 3, HD), 0.1, 1.5, ((1, 8), (3, 4))),
        "up_fc1": bell_draw(keys[16], (NAD, R, FF), 0.1, 1.5, ((1, 8), (2, 4))),
        "down_o": bell_draw(keys[17], (NAD, R, HD), (HD // 8) ** -0.5, 0.375, ((1, 8), (2, 4))),
        "down_fc2": bell_draw(keys[18], (NAD, R, FF), FF ** -0.5, 0.0625, ((1, 8), (2, 4))),
        "up_output_factors": bell_draw(keys[19], (NAD, 2, R, MODEL_WIDTH), 0.2, 3.0, ((2, 8), (3, 4))),
    }


HIGH_PRECISION = lax.Precision.HIGHEST
GELU_C = 0.7978845608028654

@jax.custom_vjp
def lowrank_activation(v):
    return lax.optimization_barrier(v.astype(jnp.bfloat16)).astype(jnp.float32)

@jax.custom_vjp
def lowrank_backward(v):
    return v

def low_keep(v):
    return (lowrank_activation(v), None)

def low_pass(kept, grad):
    return (grad,)

def back_keep(v):
    return (v, None)

def back_low(kept, grad):
    return (lowrank_activation(grad),)
lowrank_activation.defvjp(low_keep, low_pass)
lowrank_backward.defvjp(back_keep, back_low)

def gelu_tanh(values):
    return 0.5 * values * (1.0 + jnp.tanh(GELU_C * (values + 0.044715 * values * values * values)))

def angles(segments):
    places = jnp.arange(segments.shape[1], dtype=jnp.int32)
    change = jnp.concatenate([jnp.ones((segments.shape[0], 1), dtype=bool), segments[:, 1:] != segments[:, :-1]], axis=1)
    starts = lax.cummax(jnp.where(change, places[None, :], 0), axis=1)
    offsets = (places[None, :] - starts).astype(jnp.float32)
    inverse_freq = 10000.0 ** (-2.0 * jnp.arange(ROT // 2, dtype=jnp.float32) / ROT)
    phase = offsets[:, :, None, None] * inverse_freq
    return (jnp.cos(phase), jnp.sin(phase))

def rotate(tensor, cosine, sine, inverse):
    half_rot = ROT // 2
    first = tensor[..., :half_rot]
    second = tensor[..., half_rot:ROT]
    rest_dims = tensor[..., ROT:]
    if inverse:
        return jnp.concatenate([first * cosine + second * sine, second * cosine - first * sine, rest_dims], axis=-1)
    return jnp.concatenate([first * cosine - second * sine, second * cosine + first * sine, rest_dims], axis=-1)

def attend_one(packed):
    queries, keys_low, values_low, segment = packed
    scores = lowrank_backward(jnp.einsum('qhe,khe->hqk', queries, keys_low, precision=HIGH_PRECISION))
    places = jnp.arange(segment.shape[0])
    allowed = (places[None, :] <= places[:, None]) & (segment[None, :] == segment[:, None])
    scores = jnp.where(allowed[None], scores, -1e+30)
    top_score = lax.optimization_barrier(jnp.max(scores, axis=-1, keepdims=True))
    raised = jnp.exp(scores - top_score)
    probs = raised / lax.optimization_barrier(jnp.sum(raised, axis=-1, keepdims=True))
    prob_low = lowrank_activation(probs)
    return lowrank_backward(lowrank_activation(jnp.einsum('hqk,khe->qhe', prob_low, values_low, precision=HIGH_PRECISION)))

def forward(hidden, adapters, segments, selected_factors, weights):
    down_input_factors, up_qkv, up_fc1, down_o, down_fc2, up_output_factors = adapters
    ln_gain, ln_bias, w_qkv, b_qkv, w_out, b_out, w_fc1, b_fc1, w_fc2, b_fc2 = weights
    mean_row = lax.optimization_barrier(jnp.mean(hidden, axis=-1, keepdims=True))
    centred = hidden - mean_row
    variance = lax.optimization_barrier(jnp.mean(centred * centred, axis=-1, keepdims=True))
    normed = lowrank_activation(centred * lax.rsqrt(variance + 1e-05) * ln_gain + ln_bias)
    normalized_sequence = normed.reshape(SEQ_DEV, LEN, MODEL_WIDTH)
    lowrank_product = lowrank_backward(lowrank_activation(jnp.einsum('mno,mgho->mngh', normalized_sequence, down_input_factors[selected_factors], precision=HIGH_PRECISION)))
    qkv_pre = jnp.dot(normed, w_qkv.reshape(MODEL_WIDTH, 3 * HD), precision=HIGH_PRECISION).reshape(SEQ_DEV, LEN, 3, HD) + b_qkv
    qkv_pre = lowrank_backward(qkv_pre + jnp.einsum('sljr,srjh->sljh', lowrank_product[:, :, :3], up_qkv[selected_factors], precision=HIGH_PRECISION))
    cosine, sine = angles(segments)
    head_shape = (SEQ_DEV, LEN, HEADS, HEAD_DIM)
    queries = lowrank_activation(rotate(qkv_pre[:, :, 0].reshape(head_shape), cosine, sine, False) * HEAD_DIM ** (-0.5))
    keys_low = lowrank_activation(rotate(qkv_pre[:, :, 1].reshape(head_shape), cosine, sine, False))
    values_low = lowrank_activation(qkv_pre[:, :, 2].reshape(head_shape))
    context = lax.map(jax.checkpoint(attend_one), (queries, keys_low, values_low, segments))
    context = context.reshape(TOKENS_PER_SHARD, HD)
    fc1_extra = jnp.einsum('slr,srf->slf', lowrank_product[:, :, 3], up_fc1[selected_factors], precision=HIGH_PRECISION).reshape(TOKENS_PER_SHARD, FF)
    fc1_pre = lowrank_backward(jnp.dot(normed, w_fc1, precision=HIGH_PRECISION) + b_fc1 + fc1_extra)
    activated = lowrank_activation(gelu_tanh(fc1_pre))
    context_seq = context.reshape(SEQ_DEV, LEN, HD)
    active_seq = activated.reshape(SEQ_DEV, LEN, FF)
    branch_lowrank = lowrank_backward(lowrank_activation(jnp.stack([jnp.einsum('slh,srh->slr', context_seq, down_o[selected_factors], precision=HIGH_PRECISION), jnp.einsum('slf,srf->slr', active_seq, down_fc2[selected_factors], precision=HIGH_PRECISION)], axis=2)))
    adapter_output = jnp.einsum('fupz,fpzk->fuk', branch_lowrank, up_output_factors[selected_factors], precision=HIGH_PRECISION).reshape(TOKENS_PER_SHARD, MODEL_WIDTH)
    return hidden + jnp.dot(context, w_out, precision=HIGH_PRECISION) + b_out + jnp.dot(activated, w_fc2, precision=HIGH_PRECISION) + b_fc2 + adapter_output

def widen(array):
    return array.astype(jnp.float32)

def reference(hidden_in, cotangent, segment_ids, adapter_ids, ln_gain, ln_bias, w_qkv, b_qkv, w_out, b_out, w_fc1, b_fc1, w_fc2, b_fc2, down_input_factors, up_qkv, up_fc1, down_o, down_fc2, up_output_factors):
    adapters = tuple((widen(array) for array in (down_input_factors, up_qkv, up_fc1, down_o, down_fc2, up_output_factors)))
    weights = tuple((widen(array) for array in (ln_gain, ln_bias, w_qkv, b_qkv, w_out, b_out, w_fc1, b_fc1, w_fc2, b_fc2)))
    hidden_groups = widen(hidden_in).reshape(N_DP, TOKENS_PER_SHARD, MODEL_WIDTH)
    cot_groups = widen(cotangent).reshape(N_DP, TOKENS_PER_SHARD, MODEL_WIDTH)
    seg_groups = segment_ids.reshape(N_DP, SEQ_DEV, LEN)
    id_groups = adapter_ids.reshape(N_DP, SEQ_DEV)

    def one_group(totals, group):
        hidden, cot_rows, segments, selected_factors = group

        def closed(hidden_var, adapter_var):
            return forward(hidden_var, adapter_var, segments, selected_factors, weights)
        result, pullback = jax.vjp(closed, hidden, adapters)
        grad_hidden, grad_adapters = pullback(cot_rows)
        totals = jax.tree.map(jnp.add, totals, grad_adapters)
        return (totals, (result.astype(jnp.bfloat16), grad_hidden.astype(jnp.bfloat16)))
    zero_init = jax.tree.map(jnp.zeros_like, adapters)
    totals, (results, grads) = lax.scan(one_group, zero_init, (hidden_groups, cot_groups, seg_groups, id_groups))
    return (results.reshape(TOKENS, MODEL_WIDTH), grads.reshape(TOKENS, MODEL_WIDTH), totals[0], totals[1], totals[2], totals[3], totals[4], totals[5])
```

```python
import jax
import jax.numpy as jnp
from jax import lax
from jax.experimental import pallas as pl
from jax.experimental.pallas import tpu as pltpu
from jax.sharding import PartitionSpec as P

MODEL_WIDTH = 2048
HEAD_DIM = 64
ROT = 32
NAD = 8
LEN = 1024
RANK = 16


EPSILON = 1e-05
GELU_C = 0.7978845608028654
SUMMATION_DTYPE = jnp.float32


def doc_starts(segments):
    places = jnp.arange(segments.shape[1], dtype=jnp.int32)
    change = jnp.concatenate(
        [jnp.ones((segments.shape[0], 1), dtype=bool), segments[:, 1:] != segments[:, :-1]], axis=1
    )
    return lax.cummax(jnp.where(change, places[None, :], 0), axis=1)


def turn_table(starts):
    places = jnp.arange(starts.shape[1], dtype=jnp.int32)
    offsets = (places[None, :] - starts).astype(jnp.float32).reshape(-1, 1)
    inverse_freq = 10000.0 ** (-2.0 * jnp.arange(ROT // 2, dtype=jnp.float32) / ROT)
    phase = offsets * inverse_freq
    cosine, sine = jnp.cos(phase), jnp.sin(phase)
    rest = jnp.ones((phase.shape[0], HEAD_DIM - ROT), jnp.float32)
    none, zero = jnp.zeros_like(rest), jnp.zeros_like(sine)
    heads = PAIR // HEAD_DIM
    return jnp.stack(
        [
            jnp.concatenate([cosine, cosine, rest] * heads, axis=1),
            jnp.concatenate([sine, zero, none] * heads, axis=1),
            jnp.concatenate([zero, sine, none] * heads, axis=1),
        ]
    )


PAIR = 2 * HEAD_DIM
BLOCK_Q = 256
REACH = 512


def spans():
    for start in range(0, LEN, BLOCK_Q):
        yield start, max(0, start - REACH), start + BLOCK_Q


def masked_exp_args(score, doc_ref, start, low, high):
    keys = lax.broadcasted_iota(jnp.int32, (high - low, BLOCK_Q), 0) + low
    asks = lax.broadcasted_iota(jnp.int32, (high - low, BLOCK_Q), 1) + start
    first = doc_ref[0, :, start : start + BLOCK_Q]
    return jnp.where((keys >= first) & (keys <= asks), score, -1e30)


def dot_tt(left, right):
    return lax.dot_general(
        left, right, (((1,), (1,)), ((), ())), preferred_element_type=SUMMATION_DTYPE
    )


def head_only(rows, head):
    lanes = lax.broadcasted_iota(jnp.int32, rows.shape, 1)
    return jnp.where(lanes // HEAD_DIM == head, rows, jnp.zeros_like(rows))


def attend_kernel(doc_ref, q_ref, k_ref, v_ref, out_ref, log_ref):
    values_t = v_ref[...].astype(jnp.float32).T.astype(jnp.bfloat16)
    for start, low, high in spans():
        parts = []
        for head in range(2):
            ask = head_only(q_ref[start : start + BLOCK_Q, :], head)
            score = masked_exp_args(dot_tt(k_ref[low:high, :], ask), doc_ref, start, low, high)
            top = jnp.max(score, axis=0, keepdims=True)
            raised = jnp.exp(score - top)
            total = jnp.sum(raised, axis=0, keepdims=True)
            mix = jnp.dot(
                values_t[head * HEAD_DIM : (head + 1) * HEAD_DIM, low:high],
                raised.astype(jnp.bfloat16),
                preferred_element_type=SUMMATION_DTYPE,
            )
            parts.append(mix / total)
            log_ref[0, 0, head : head + 1, start : start + BLOCK_Q] = top + jnp.log(total)
        out_ref[start : start + BLOCK_Q, :] = jnp.concatenate(parts, axis=0).T.astype(jnp.bfloat16)


def turn(rows, table_ref, inverse):
    half = ROT // 2
    wide = rows.shape[1]
    plus = pltpu.roll(rows, wide - half, axis=1)
    minus = pltpu.roll(rows, half, axis=1)
    cosine, first_sine, second_sine = table_ref[0], table_ref[1], table_ref[2]
    if inverse:
        return rows * cosine + plus * first_sine - minus * second_sine
    return rows * cosine - plus * first_sine + minus * second_sine


def attend_back_kernel(
    doc_ref, q_ref, k_ref, v_ref, g_ref, log_ref, table_ref, dq_ref, dk_ref, dv_ref,
    sum_q, sum_k, sum_v,
):
    keys_t = k_ref[...].astype(jnp.float32).T.astype(jnp.bfloat16)
    sum_k[...] = jnp.zeros_like(sum_k)
    sum_v[...] = jnp.zeros_like(sum_v)
    for start, low, high in spans():
        here = slice(start, start + BLOCK_Q)
        for head in range(2):
            ask = head_only(q_ref[here, :], head)
            grad = head_only(g_ref[here, :], head)
            score = masked_exp_args(dot_tt(k_ref[low:high, :], ask), doc_ref, start, low, high)
            probs = jnp.exp(score - log_ref[0, 0, head : head + 1, here])
            grad_probs = dot_tt(v_ref[low:high, :], grad)
            delta = jnp.sum(probs * grad_probs, axis=0, keepdims=True)
            grad_score = (probs * (grad_probs - delta)).astype(jnp.bfloat16)
            sum_v[low:high, :] += jnp.dot(
                probs.astype(jnp.bfloat16), grad, preferred_element_type=SUMMATION_DTYPE
            )
            sum_k[low:high, :] += jnp.dot(
                grad_score, ask, preferred_element_type=SUMMATION_DTYPE
            )
            sum_q[head * HEAD_DIM : (head + 1) * HEAD_DIM, here] = jnp.dot(
                keys_t[head * HEAD_DIM : (head + 1) * HEAD_DIM, low:high],
                grad_score,
                preferred_element_type=SUMMATION_DTYPE,
            )
    scale = HEAD_DIM ** (-0.5)
    dq_ref[...] = turn(sum_q[...].T * scale, table_ref, True).astype(jnp.bfloat16)
    dk_ref[...] = turn(sum_k[...], table_ref, True).astype(jnp.bfloat16)
    dv_ref[...] = sum_v[...].astype(jnp.bfloat16)


def attention_specs(seq_count, pairs):
    rows = pl.BlockSpec((LEN, PAIR), lambda s, p: (s, p))
    doc = pl.BlockSpec((1, 1, LEN), lambda s, p: (s, 0, 0))
    logs = pl.BlockSpec((1, 1, 2, LEN), lambda s, p: (s, p, 0, 0))
    table = pl.BlockSpec((3, LEN, PAIR), lambda s, p: (0, s, 0))
    return rows, doc, logs, table


def attention(doc, queries, keys, values):
    seq_count = doc.shape[0]
    pairs = queries.shape[1] // PAIR
    rows, docs, logs, _ = attention_specs(seq_count, pairs)
    area = seq_count * pairs * 2 * 9 * BLOCK_Q * BLOCK_Q
    return pl.pallas_call(
        attend_kernel,
        grid=(seq_count, pairs),
        in_specs=[docs, rows, rows, rows],
        out_specs=[rows, logs],
        out_shape=[
            jax.ShapeDtypeStruct(queries.shape, jnp.bfloat16),
            jax.ShapeDtypeStruct((seq_count, pairs, 2, LEN), jnp.float32),
        ],
        cost_estimate=pl.CostEstimate(
            flops=area * 4 * PAIR, bytes_accessed=queries.size * 8, transcendentals=area
        ),
        name="attend",
    )(doc, queries, keys, values)


def attention_back(doc, queries, keys, values, grad, logs_in, table):
    seq_count = doc.shape[0]
    pairs = queries.shape[1] // PAIR
    rows, docs, logs, tables = attention_specs(seq_count, pairs)
    area = seq_count * pairs * 2 * 9 * BLOCK_Q * BLOCK_Q
    return pl.pallas_call(
        attend_back_kernel,
        grid=(seq_count, pairs),
        in_specs=[docs, rows, rows, rows, rows, logs, tables],
        out_specs=[rows, rows, rows],
        out_shape=[jax.ShapeDtypeStruct(queries.shape, jnp.bfloat16)] * 3,
        scratch_shapes=[
            pltpu.VMEM((PAIR, LEN), jnp.float32),
            pltpu.VMEM((LEN, PAIR), jnp.float32),
            pltpu.VMEM((LEN, PAIR), jnp.float32),
        ],
        cost_estimate=pl.CostEstimate(
            flops=area * 10 * PAIR, bytes_accessed=queries.size * 14, transcendentals=area
        ),
        name="attend_back",
    )(doc, queries, keys, values, grad, logs_in, table)


def ring_order(count):
    inner = 2 if count <= 8 else 4
    outer = max(count // inner, 1)
    if count % inner:
        return list(range(count))
    order = [z * inner for z in range(outer)]
    for z in range(outer - 1, -1, -1):
        rest = list(range(1, inner))
        if (outer - 1 - z) % 2:
            rest = rest[::-1]
        order += [z * inner + y for y in rest]
    return order


def ring_gather(block, count, axis, rows):
    order = ring_order(count)
    place = [order.index(i) for i in range(count)]
    ahead = [(order[i], order[(i + 1) % count]) for i in range(count)]
    back = [(b, a) for a, b in ahead]
    me = jnp.asarray(place, jnp.int32)[lax.axis_index("dp")]
    table = jnp.asarray(order, jnp.int32)
    half = block.shape[rows] // 2
    size = block.shape[axis]
    shape = list(block.shape)
    shape[axis] = size * count
    out = jnp.zeros(shape, block.dtype)
    down, up = count // 2, count - 1 - count // 2
    found = []
    for part in range(2):
        piece = lax.slice_in_dim(block, part * half, (part + 1) * half, axis=rows)
        found.append((part, 0, piece))
        for route, sign, hops in ((ahead, -1, (down, up)[part]), (back, 1, (up, down)[part])):
            moving = piece
            for hop in range(1, hops + 1):
                moving = lax.ppermute(moving, "dp", route)
                found.append((part, sign * hop, moving))
    for part, shift, piece in sorted(found, key=lambda f: abs(f[1])):
        source = table[lax.rem(me + shift + count, count)]
        start = [0] * block.ndim
        start[rows] = part * half
        start[axis] = start[axis] + source * size
        out = lax.dynamic_update_slice(out, piece, start)
    return out


def swap(value, axis, count, bit):
    return lax.ppermute(value, axis, [(i, i ^ bit) for i in range(count)])


def bits_of(count):
    return [1 << b for b in range(count.bit_length() - 1)]


def pieces_of(block, count):
    pieces = {0: block}
    for bit in reversed(bits_of(count)):
        for key in list(pieces):
            pieces[key ^ bit] = swap(pieces[key], "mp", count, bit)
    return [pieces[k] for k in range(count)]


def lay_out(pieces, axis):
    me = lax.axis_index("mp")
    size = pieces[0].shape[axis]
    out = jnp.concatenate(pieces, axis=axis)
    for key, piece in enumerate(pieces):
        out = lax.dynamic_update_slice_in_dim(out, piece, (me ^ key) * size, axis=axis)
    return out


def sum_over_mp(value, count):
    for bit in bits_of(count):
        value = value + swap(value, "mp", count, bit)
    return value


def share_out(partial, count):
    me = lax.axis_index("mp")
    width = partial.shape[1] // count
    kept = partial
    for bit in bits_of(count):
        ahead = kept.shape[1] // (2 * width)
        mine = lax.rem(me // bit, 2)
        grid = kept.reshape(kept.shape[0], ahead, 2, width)
        give = lax.dynamic_index_in_dim(grid, 1 - mine, 2, keepdims=False)
        keep = lax.dynamic_index_in_dim(grid, mine, 2, keepdims=False)
        got = swap(give.reshape(-1, ahead * width).astype(jnp.bfloat16), "mp", count, bit)
        kept = keep.reshape(-1, ahead * width) + got.astype(jnp.float32)
    return kept


def shift_dp(value, count, shift):
    return lax.ppermute(value, "dp", [(i, (i + shift) % count) for i in range(count)])


def in_order(received, count):
    rolled = jnp.stack(received[::-1] * 2)
    start = count - 1 - lax.axis_index("dp")
    return lax.dynamic_slice_in_dim(rolled, start, count, axis=0)


def one_hot(ids):
    return (ids[:, None] == jnp.arange(NAD, dtype=jnp.int32)[None, :]).astype(jnp.bfloat16)


def dot(left, right):
    return jnp.dot(left, right, preferred_element_type=SUMMATION_DTYPE)


def sums(spec, left, right):
    return jnp.einsum(spec, left, right, preferred_element_type=SUMMATION_DTYPE)


def gelu_tanh(values):
    return 0.5 * values * (1.0 + jnp.tanh(GELU_C * (values + 0.044715 * values * values * values)))


def gelu_slope(values):
    square = values * values
    bend = jnp.tanh(GELU_C * (values + 0.044715 * values * square))
    return 0.5 * (1.0 + bend) + 0.5 * values * (1.0 - bend * bend) * (
        GELU_C * (1.0 + 3.0 * 0.044715 * square)
    )


def turned(rows, table, heads):
    half = ROT // 2
    cosine, first_sine, second_sine = [
        jnp.concatenate([t] * (heads * HEAD_DIM // PAIR), axis=1) for t in table
    ]
    plus = jnp.roll(rows, -half, axis=1)
    minus = jnp.roll(rows, half, axis=1)
    return rows * cosine - plus * first_sine + minus * second_sine


def make_body(n_dp, n_mp):
    def body(
        hidden_in, cotangent, segment_ids, adapter_ids, ln_gain, ln_bias, w_qkv, b_qkv, w_out,
        b_out, w_fc1, b_fc1, w_fc2, b_fc2, down_input_factors, up_qkv, up_fc1, down_o, down_fc2,
        up_output_factors,
    ):
        seqs = adapter_ids.shape[0]
        tokens = hidden_in.shape[0]
        head_cols = b_qkv.shape[1]
        ff_cols = b_fc1.shape[0]
        width = b_out.shape[0]
        ranks = up_fc1.shape[1]
        features = down_input_factors.shape[3]
        me = lax.axis_index("mp")

        ids = [adapter_ids] + [shift_dp(adapter_ids, n_dp, k) for k in range(1, n_dp)]
        tables = [down_input_factors, up_qkv, up_fc1, down_o, down_fc2, up_output_factors]
        packed = jnp.concatenate([t.reshape(NAD, -1) for t in tables], axis=1)
        asked = jnp.concatenate([ids[(n_dp - k) % n_dp] for k in range(n_dp)])
        picked = dot(one_hot(asked), packed).astype(jnp.bfloat16).reshape(n_dp, seqs, -1)
        got = [picked[0]] + [shift_dp(picked[k], n_dp, k) for k in range(1, n_dp)]
        mine = in_order(got, n_dp)
        cut, spot = [], 0
        for t in tables:
            size = t.size // NAD
            cut.append(mine[:, :, spot : spot + size].reshape((n_dp, seqs) + t.shape[1:]))
            spot += size
        rank = n_dp * ranks
        a_in = jnp.moveaxis(cut[0], 0, 3).reshape(seqs, 4 * rank, MODEL_WIDTH)
        u_qkv = jnp.moveaxis(cut[1], 0, 1).reshape(seqs, rank, 3, head_cols)
        u_fc1 = jnp.moveaxis(cut[2], 0, 1).reshape(seqs, rank, ff_cols)
        a_o = jnp.moveaxis(cut[3], 0, 1).reshape(seqs, rank, head_cols)
        a_fc2 = jnp.moveaxis(cut[4], 0, 1).reshape(seqs, rank, ff_cols)
        u_out = jnp.moveaxis(cut[5], 0, 2).reshape(seqs, 2 * rank, width)
        u_block = jnp.concatenate(
            [
                jnp.pad(u_qkv[:, :, j], ((0, 0), (0, 0), (j * head_cols, (2 - j) * head_cols)))
                for j in range(3)
            ],
            axis=1,
        )

        hidden_full = lay_out(pieces_of(hidden_in, n_mp), 1)
        wide_qkv = ring_gather(w_qkv.reshape(features, 3 * head_cols), n_dp, 0, 0)
        cot_full = lay_out(pieces_of(cotangent, n_mp), 1)
        wide_out = ring_gather(w_out, n_dp, 1, 0)
        wide_fc1 = lax.all_gather(w_fc1, "dp", axis=0, tiled=True)
        wide_fc2 = lax.all_gather(w_fc2, "dp", axis=1, tiled=True)

        def by_seq(rows):
            return rows.reshape(seqs, LEN, rows.shape[1])

        starts = doc_starts(segment_ids)
        table = turn_table(starts)
        doc = starts[:, None, :]
        cot_seq = by_seq(cotangent)
        back_sum = sum_over_mp(sums("slh,srh->srl", cot_seq, u_out), n_mp)
        back_low = back_sum.astype(jnp.bfloat16)

        wide_in = hidden_full.astype(jnp.float32)
        mean_row = jnp.mean(wide_in, axis=-1, keepdims=True)
        centred = wide_in - mean_row
        inv_std = lax.rsqrt(jnp.mean(centred * centred, axis=-1, keepdims=True) + EPSILON)
        normed = (centred * inv_std * ln_gain + ln_bias).astype(jnp.bfloat16)
        normed_seq = by_seq(normed)
        low = sums("slm,srm->srl", normed_seq, a_in).astype(jnp.bfloat16)
        qkv_pre = (
            dot(normed, wide_qkv)
            + b_qkv.reshape(-1).astype(jnp.float32)
            + sums("srl,srh->slh", low[:, : 3 * rank], u_block).reshape(tokens, 3 * head_cols)
        )
        heads = head_cols // HEAD_DIM
        queries = (
            turned(qkv_pre[:, :head_cols], table, heads) * HEAD_DIM ** (-0.5)
        ).astype(jnp.bfloat16)
        keys = turned(qkv_pre[:, head_cols : 2 * head_cols], table, heads).astype(jnp.bfloat16)
        values = qkv_pre[:, 2 * head_cols :].astype(jnp.bfloat16)
        context, logs = attention(doc, queries, keys, values)

        grad_context = (
            lax.dot_general(
                cot_full, wide_out, (((1,), (1,)), ((), ())), preferred_element_type=SUMMATION_DTYPE
            )
            + sums("srl,srh->slh", back_low[:, :rank], a_o).reshape(tokens, head_cols)
        ).astype(jnp.bfloat16)
        grad_q, grad_k, grad_v = attention_back(
            doc, queries, keys, values, grad_context, logs, table
        )
        grad_qkv = jnp.concatenate([grad_q, grad_k, grad_v], axis=1)

        fc1_pre = (
            dot(normed, wide_fc1)
            + b_fc1.astype(jnp.float32)
            + sums("srl,srf->slf", low[:, 3 * rank :], u_fc1).reshape(tokens, ff_cols)
        )
        activated = gelu_tanh(fc1_pre).astype(jnp.bfloat16)
        slope = gelu_slope(fc1_pre).astype(jnp.bfloat16)
        grad_active = lax.dot_general(
            cot_full, wide_fc2, (((1,), (1,)), ((), ())), preferred_element_type=SUMMATION_DTYPE
        ) + sums("srl,srf->slf", back_low[:, rank:], a_fc2).reshape(tokens, ff_cols)
        grad_fc1 = (grad_active * slope.astype(jnp.float32)).astype(jnp.bfloat16)

        branch_sum = sum_over_mp(
            jnp.concatenate(
                [
                    sums("slh,srh->srl", by_seq(context), a_o),
                    sums("slf,srf->srl", by_seq(activated), a_fc2),
                ],
                axis=1,
            ),
            n_mp,
        )
        branch_low = branch_sum.astype(jnp.bfloat16)
        mixed = share_out(dot(context, wide_out) + dot(activated, wide_fc2), n_mp)
        output = (
            hidden_in.astype(jnp.float32)
            + mixed
            + b_out.astype(jnp.float32)
            + b_fc2.astype(jnp.float32)
            + sums("srl,srk->slk", branch_low, u_out).reshape(tokens, width)
        ).astype(jnp.bfloat16)

        rank_sum = sum_over_mp(
            jnp.concatenate(
                [
                    sums("slh,srh->srl", by_seq(grad_qkv), u_block),
                    sums("slf,srf->srl", by_seq(grad_fc1), u_fc1),
                ],
                axis=1,
            ),
            n_mp,
        )
        rank_low = rank_sum.astype(jnp.bfloat16)

        partial = lax.dot_general(
            grad_qkv, wide_qkv, (((1,), (1,)), ((), ())), preferred_element_type=SUMMATION_DTYPE
        ) + lax.dot_general(
            grad_fc1, wide_fc1, (((1,), (1,)), ((), ())), preferred_element_type=SUMMATION_DTYPE
        )
        a_mine = lax.dynamic_slice_in_dim(a_in, me * width, width, axis=2)
        gain = lax.dynamic_slice_in_dim(ln_gain, me * width, width)
        grad_normed = share_out(partial, n_mp) + sums("srl,srk->slk", rank_low, a_mine).reshape(
            tokens, width
        )
        scaled = grad_normed * gain
        x_hat = (hidden_in.astype(jnp.float32) - mean_row) * inv_std
        row_sums = sum_over_mp(
            jnp.stack([jnp.sum(scaled, axis=1), jnp.sum(scaled * x_hat, axis=1)]), n_mp
        ) / MODEL_WIDTH
        grad_in = (
            cotangent.astype(jnp.float32)
            + inv_std * (scaled - row_sums[0][:, None] - x_hat * row_sums[1][:, None])
        ).astype(jnp.bfloat16)

        share = 4 * rank // n_mp
        rank_mine = lax.dynamic_slice_in_dim(rank_low, me * share, share, axis=1)
        g_in = sums("srl,slm->srm", rank_mine, normed_seq)
        g_qkv = jnp.stack(
            [
                sums("srl,slh->srh", low[:, j * rank : (j + 1) * rank], by_seq(g))
                for j, g in enumerate((grad_q, grad_k, grad_v))
            ],
            axis=2,
        )
        g_fc1 = sums("srl,slf->srf", low[:, 3 * rank :], by_seq(grad_fc1))
        g_o = sums("srl,slh->srh", back_low[:, :rank], by_seq(context))
        g_fc2 = sums("srl,slf->srf", back_low[:, rank:], by_seq(activated))
        g_out = sums("srl,slk->srk", branch_low, cot_seq)
        sends = [
            jnp.moveaxis(g_in.reshape(seqs, share, n_dp, features), 2, 0),
            jnp.moveaxis(g_qkv.reshape(seqs, n_dp, ranks, 3, head_cols), 1, 0),
            jnp.moveaxis(g_fc1.reshape(seqs, n_dp, ranks, ff_cols), 1, 0),
            jnp.moveaxis(g_o.reshape(seqs, n_dp, ranks, head_cols), 1, 0),
            jnp.moveaxis(g_fc2.reshape(seqs, n_dp, ranks, ff_cols), 1, 0),
            jnp.moveaxis(g_out.reshape(seqs, 2, n_dp, ranks, width), 2, 0),
        ]
        shapes = [s.shape[2:] for s in sends]
        for_peer = jnp.concatenate(
            [s.reshape(n_dp, seqs, -1) for s in sends], axis=2
        ).astype(jnp.bfloat16)
        here = lax.axis_index("dp")
        arrived = []
        for k in range(n_dp):
            piece = lax.dynamic_index_in_dim(
                for_peer, lax.rem(here + k, n_dp), 0, keepdims=False
            )
            arrived.append(shift_dp(piece, n_dp, k) if k else piece)
        owned = lax.dot_general(
            one_hot(jnp.concatenate(ids)),
            jnp.concatenate(arrived, axis=0),
            (((0,), (0,)), ((), ())),
            preferred_element_type=SUMMATION_DTYPE,
        )
        outs, spot = [], 0
        for shape in shapes:
            size = 1
            for n in shape:
                size *= n
            outs.append(owned[:, spot : spot + size].reshape((NAD,) + shape))
            spot += size
        grad_down_x = lay_out(pieces_of(outs[0], n_mp), 1).reshape(NAD, 4, rank, features)
        return (output, grad_in, grad_down_x, *outs[1:])

    return body


def solution(mesh):
    in_specs = (
        P("dp", "mp"),
        P("dp", "mp"),
        P("dp", None),
        P("dp"),
        P(),
        P(),
        P("dp", None, "mp"),
        P(None, "mp"),
        P("mp", "dp"),
        P("mp"),
        P("dp", "mp"),
        P("mp"),
        P("mp", "dp"),
        P("mp"),
        P(None, None, None, "dp"),
        P(None, "dp", None, "mp"),
        P(None, "dp", "mp"),
        P(None, "dp", "mp"),
        P(None, "dp", "mp"),
        P(None, None, "dp", "mp"),
    )
    out_specs = (
        P("dp", "mp"),
        P("dp", "mp"),
        P(None, None, None, "dp"),
        P(None, "dp", None, "mp"),
        P(None, "dp", "mp"),
        P(None, "dp", "mp"),
        P(None, "dp", "mp"),
        P(None, None, "dp", "mp"),
    )
    return jax.shard_map(
        make_body(mesh.shape["dp"], mesh.shape["mp"]), mesh=mesh, in_specs=in_specs, out_specs=out_specs, check_vma=False)
```
